512 devices in a mesh: dp: 8 (over y, core), row: 64 (over x, z).
Axes of the slice: x: 4, y: 4, z: 16, core: 2. Of those that a mesh axis runs over, the one named last changes fastest.
Arguments:
- hidden: bfloat16 [8, 128, 128, 768], P('dp', 'row'), may hold values from -6 to 6
- masked: int32 [8, 128, 128], P('dp', 'row'), may hold values 0 or 1
- depths: int32 [8], P('dp'), may hold values from 32 to 128, as said below
- norm_gain: float32 [768], replicated, may hold values from 0.25 to 1.75
- w_query: bfloat16 [768, 768], P('row'), may hold values from -0.21875 to 0.21875
- w_key: bfloat16 [768, 768], P('row'), may hold values from -0.21875 to 0.21875
- w_value: bfloat16 [768, 768], P('row'), may hold values from -0.21875 to 0.21875
- w_out: bfloat16 [768, 768], P('row'), may hold values from -0.21875 to 0.21875
- cotangent: bfloat16 [8, 128, 128, 768], P('dp', 'row'), may hold values from -6 to 6
Outputs:
- mixed: bfloat16 [8, 128, 128, 768], P('dp', 'row')
- grad_hidden: bfloat16 [8, 128, 128, 768], P('dp', 'row')
The draws below stay inside these ranges and needn't reach their ends.
Inputs may be any that keep to these rules, and one draw needn't show every extreme that they name: `depths`: rows at or past an MSA's depth are padding.
All inputs are finite; a program needn't handle non-finite values. No bound on the sum of `masked` on one device may be relied on, other than what follows from the above.
Results may differ from the reference program's by a relative error of at most 0.0059.
Values may be sent and summed in bfloat16 or wider, within the bound.
A program may use at most 64 MiB of HBM per device.

```python
import jax
import jax.numpy as jnp
from jax import lax

D = 768
HEADS = 12
HEAD_DIM = 64
COLS = 128
ROWS = 128
GROUPS = 8


def draw_depths(key, part):
    base_key = jax.random.fold_in(key, 11)
    first_key, second_key = jax.random.split(base_key)
    base = jax.random.randint(first_key, (GROUPS,), ROWS // 4, ROWS + 1).astype(jnp.int32)
    order = jax.random.permutation(second_key, GROUPS)
    base = base.at[order[0]].set(ROWS)
    base = base.at[order[1]].set(ROWS // 4)
    return base.astype(jnp.int32)


def with_ends(drawn, stream_key, least, high):
    extent = drawn.shape
    spot = [jax.random.randint(jax.random.fold_in(stream_key, axis), (), 0, extent[axis]) for axis in range(len(extent))]
    drawn = drawn.at[tuple(spot)].set(least)
    longest = extent.index(max(extent))
    spot[longest] = (spot[longest] + 1) % extent[longest]
    return drawn.at[tuple(spot)].set(high)


def level_of(rng, shape, shards, low, largest):
    loudness, own = 1.0, jax.random.fold_in(rng, 6)
    for axis_at, blocks in shards:
        draws = jnp.exp(jax.random.uniform(jax.random.fold_in(own, axis_at), (blocks,), jnp.float32, low / len(shards), largest / len(shards)))
        loudness = loudness * jnp.repeat(draws, shape[axis_at] // blocks).reshape([-1 if axis == axis_at else 1 for axis in range(len(shape))])
    return loudness


def scatter_about(own_key, extent, spread, bound, cuts=(), held_as=jnp.bfloat16):
    drawn = spread * jax.random.normal(own_key, extent, jnp.float32)
    if cuts:
        drawn = drawn * level_of(own_key, extent, cuts, -0.22, 0.18)
    return jnp.clip(drawn, -bound, bound).astype(held_as)


def setup_inputs(seed: int = 0) -> dict:
    seeds = jax.random.split(jax.random.key(seed), 10)
    hidden = scatter_about(seeds[0], (GROUPS, ROWS, COLS, D), 1.0, 6.0, ((0, 8), (1, 64)))
    masked = with_ends((jax.random.randint(seeds[1], (GROUPS, ROWS, COLS), 0, 4) < 1).astype(jnp.int32), jax.random.fold_in(seeds[1], 1), 0, 1)
    depths = draw_depths(jax.random.fold_in(seeds[9], 71), 0)
    norm_gain = jnp.clip(1.0 + 0.15 * jax.random.normal(seeds[3], (D,), jnp.float32), 0.25, 1.75)
    w_query = scatter_about(seeds[4], (D, D), D ** -0.5, 0.21875, ((0, 64),))
    w_key = scatter_about(seeds[5], (D, D), D ** -0.5, 0.21875, ((0, 64),))
    w_value = scatter_about(seeds[6], (D, D), D ** -0.5, 0.21875, ((0, 64),))
    w_out = scatter_about(seeds[7], (D, D), D ** -0.5, 0.21875, ((0, 64),))
    cotangent = scatter_about(seeds[8], (GROUPS, ROWS, COLS, D), 1.0, 6.0, ((0, 8), (1, 64)))
    return {"hidden": hidden, "masked": masked, "depths": depths, "norm_gain": norm_gain, "w_query": w_query, "w_key": w_key, "w_value": w_value, "w_out": w_out, "cotangent": cotangent}


EPS = 1e-05

def softmax_rows(scores):
    top = lax.optimization_barrier(jnp.max(scores, axis=-1, keepdims=True))
    expo = jnp.exp(scores - top)
    return expo / lax.optimization_barrier(jnp.sum(expo, axis=-1, keepdims=True))

def group_pass(hidden_rows, mask_rows, depth, cot_rows, loss_ratio, norm_gain, w_query, w_key, w_value, w_out):
    slots = jnp.arange(ROWS).astype(jnp.int32)
    alive = (slots < depth).astype(jnp.float32)
    widened = hidden_rows.astype(jnp.float32)
    average = lax.optimization_barrier(jnp.mean(widened, axis=-1, keepdims=True))
    centred = widened - average
    variance = lax.optimization_barrier(jnp.mean(centred * centred, axis=-1, keepdims=True))
    inv_std = lax.rsqrt(variance + EPS)
    x_hat = centred * inv_std
    normed = (x_hat * norm_gain).astype(jnp.bfloat16).reshape(ROWS * COLS, D)

    def project(weight):
        out = jnp.dot(normed, weight, preferred_element_type=jnp.float32).astype(jnp.bfloat16)
        return out.reshape(ROWS, COLS, HEADS, HEAD_DIM)
    queries = project(w_query)
    keys_proj = project(w_key)
    values_proj = project(w_value)
    scale = 1.0 / jnp.sqrt(depth.astype(jnp.float32) * HEAD_DIM)
    query_live = queries.astype(jnp.float32) * alive[:, None, None, None]
    keys_wide = keys_proj.astype(jnp.float32)
    values_wide = values_proj.astype(jnp.float32)
    logits = jnp.einsum('rihe,rjhe->hij', query_live, keys_wide) * scale
    probs = softmax_rows(logits)
    probs_low = probs.astype(jnp.bfloat16)
    attended = jnp.einsum('hij,rjhe->rihe', probs_low.astype(jnp.float32), values_wide).astype(jnp.bfloat16)
    projected = jnp.dot(attended.reshape(ROWS * COLS, D), w_out, preferred_element_type=jnp.float32)
    mixed = (widened + alive[:, None, None] * projected.reshape(ROWS, COLS, D)).astype(jnp.bfloat16)
    weighting = mask_rows.astype(jnp.float32) * alive[:, None] * loss_ratio
    grad_mixed = cot_rows.astype(jnp.float32) * weighting[:, :, None]
    grad_low = grad_mixed.astype(jnp.bfloat16).reshape(ROWS * COLS, D)
    grad_attended = jnp.dot(grad_low, w_out.T, preferred_element_type=jnp.float32).astype(jnp.bfloat16)
    grad_att_wide = grad_attended.reshape(ROWS, COLS, HEADS, HEAD_DIM).astype(jnp.float32)
    grad_probs = jnp.einsum('rihe,rjhe->hij', grad_att_wide, values_wide)
    grad_values = jnp.einsum('hij,rihe->rjhe', probs_low.astype(jnp.float32), grad_att_wide).astype(jnp.bfloat16)
    grad_logits = probs * (grad_probs - lax.optimization_barrier(jnp.sum(probs * grad_probs, axis=-1, keepdims=True)))
    grad_logits = (grad_logits * scale).astype(jnp.bfloat16).astype(jnp.float32)
    grad_queries = (jnp.einsum('hij,rjhe->rihe', grad_logits, keys_wide) * alive[:, None, None, None]).astype(jnp.bfloat16)
    grad_keys = jnp.einsum('hij,rihe->rjhe', grad_logits, query_live).astype(jnp.bfloat16)
    grad_normed = jnp.dot(grad_queries.reshape(ROWS * COLS, D), w_query.T, preferred_element_type=jnp.float32)
    grad_normed = grad_normed + jnp.dot(grad_keys.reshape(ROWS * COLS, D), w_key.T, preferred_element_type=jnp.float32)
    grad_normed = grad_normed + jnp.dot(grad_values.reshape(ROWS * COLS, D), w_value.T, preferred_element_type=jnp.float32)
    scaled = grad_normed.reshape(ROWS, COLS, D) * norm_gain
    grad_x = inv_std * (scaled - lax.optimization_barrier(jnp.mean(scaled, axis=-1, keepdims=True)) - x_hat * lax.optimization_barrier(jnp.mean(scaled * x_hat, axis=-1, keepdims=True)))
    grad_hidden = (grad_mixed + grad_x).astype(jnp.bfloat16)
    return (mixed, grad_hidden)

def reference(hidden, masked, depths, norm_gain, w_query, w_key, w_value, w_out, cotangent):
    slots = jnp.arange(ROWS).astype(jnp.int32)
    alive_all = (slots[None, :] < depths[:, None]).astype(jnp.float32)
    live_total = jnp.sum(alive_all) * COLS
    masked_total = jnp.sum(masked.astype(jnp.float32) * alive_all[:, :, None])
    loss_ratio = live_total / jnp.maximum(masked_total, 1.0)

    def one_group(item):
        hidden_rows, mask_rows, depth, cot_rows = item
        return group_pass(hidden_rows, mask_rows, depth, cot_rows, loss_ratio, norm_gain, w_query, w_key, w_value, w_out)
    mixed, grad_hidden = lax.map(one_group, (hidden, masked, depths, cotangent))
    return (mixed, grad_hidden)
```

```python
import jax
import jax.numpy as jnp
from jax import lax
from jax.experimental import pallas as pl
from jax.experimental.pallas import tpu as pltpu
from jax.sharding import PartitionSpec as P

HEADS = 12
EPS = 1e-05
NX, NY, NZ, NC = 4, 4, 16, 2
D = 768
COLS = 128
SHARD = D // (NX * NZ)
SLAB = SHARD * NZ
HALF = D // NC
HPX = HEADS // NX
IPZ = COLS // NZ
CHUNK = 2 * HPX * IPZ
MESH = pl.DeviceIdType.MESH
BF, F32 = jnp.bfloat16, jnp.float32


def place():
    dp, row = lax.axis_index("dp"), lax.axis_index("row")
    return lax.div(row, NZ), lax.div(dp, NC), lax.rem(row, NZ), lax.rem(dp, NC)


def device(x, y, z, c):
    return (y * NC + c, x * NZ + z)


def mod(a, n):
    return lax.rem(a + n, n)


class Copies:
    def __init__(self, sems):
        self.sems, self.sent = sems, []

    def send(self, src, dst, recv, to):
        copy = pltpu.make_async_remote_copy(
            src_ref=src, dst_ref=dst, send_sem=self.sems.at[len(self.sent)], recv_sem=recv,
            device_id=to, device_id_type=MESH)
        copy.start()
        self.sent.append(copy)

    def drain(self):
        for copy in self.sent:
            copy.wait_send()


def wait_recv(ref, sem):
    pltpu.make_async_copy(ref, ref, sem).wait()


def greet(devices):
    barrier = pltpu.get_barrier_semaphore()
    for to in devices:
        pl.semaphore_signal(barrier, inc=1, device_id=to, device_id_type=MESH)
    pl.semaphore_wait(barrier, len(devices))


def gather_kernel(wq, wk, wv, wo, cnt, full, total, stack, zbuf, cz, cx, cd, cy, tmp, blk,
                  local, zrecv, crecv, frecv, srecv, sibrecv, send_sems):
    x, y, z, c = place()
    loads = [pltpu.make_async_copy(w, stack.at[i], local.at[i]) for i, w in enumerate((wq, wk, wv, wo))]
    for load in loads:
        load.start()
    zs = [device(x, y, mod(z + d, NZ), c) for d in range(1, NZ)]
    xs = [device(mod(x + d, NX), y, z, c) for d in range(1, NX)]
    dps = [device(x, lax.div(e, NC), z, lax.rem(e, NC))
           for e in [mod(y * NC + c + d, NY * NC) for d in range(1, NY * NC)]]
    greet(zs + xs + dps)
    for load in loads:
        load.wait()
    copies = Copies(send_sems)
    mine = stack.at[y, :, pl.ds(pl.multiple_of(c * HALF, HALF), HALF)]
    far = sorted(range(1, NZ), key=lambda d: -min(d, NZ - d))
    for d in far:
        copies.send(mine, zbuf.at[z], zrecv, zs[d - 1])
    for d in far:
        copies.send(cnt, cz.at[z], crecv.at[0], zs[d - 1])
    keep = pltpu.make_async_copy(mine, zbuf.at[z], local.at[0])
    keep.start()
    keepc = pltpu.make_async_copy(cnt, cz.at[z], local.at[1])
    keepc.start()
    keep.wait()
    keepc.wait()
    wait_recv(zbuf.at[pl.ds(0, NZ - 1)], zrecv)
    for i in range(NZ):
        tmp[SHARD * i:SHARD * (i + 1), :] = zbuf[i].astype(F32)
    blk[...] = tmp[...].astype(BF)

    def spot(df, ds, part=None):
        bx = mod(x + df * (1 - c) + ds * c, NX)
        by = mod(y + df * c + ds * (1 - c), NY)
        first, rows = (0, SLAB) if part is None else (part * (SLAB // 2), SLAB // 2)
        return full.at[by, pl.ds(pl.multiple_of(bx * SLAB + first, 16), rows),
                       pl.ds(pl.multiple_of(c * HALF, HALF), HALF)]

    def first_to(d):
        return device(mod(x + d * (1 - c), NX), mod(y + d * c, NY), z, c)

    def second_to(d):
        return device(mod(x + d * c, NX), mod(y + d * (1 - c), NY), z, c)

    sibling = device(x, y, z, 1 - c)
    spot_own = pltpu.make_async_copy(blk, spot(0, 0), local.at[0])
    spot_own.start()
    for d, k in ((1, 0), (-1, 1)):
        copies.send(blk, spot(0, 0), frecv.at[k], first_to(d))
    for d, k in ((1, 0), (-1, 1)):
        copies.send(blk, spot(0, 0), srecv.at[0, k], second_to(d))
    copies.send(blk, spot(0, 0), sibrecv, sibling)

    wait_recv(cz.at[pl.ds(0, NZ - 1)], crecv.at[0])
    cy[0] = jnp.sum(cz[...], axis=0)
    for d in range(1, NX):
        copies.send(cy.at[0], cx.at[x], crecv.at[1], xs[d - 1])

    for k, df in ((0, -1), (1, 1)):
        wait_recv(spot(df, 0), frecv.at[k])
        copies.send(spot(df, 0, k), spot(df, 0, k), frecv.at[2 + k], first_to(-df))
        for d, j in ((1, 0), (-1, 1)):
            copies.send(spot(df, 0), spot(df, 0), srecv.at[1 + k, j], second_to(d))
        copies.send(spot(df, 0), spot(df, 0), sibrecv, sibling)

    wait_recv(cx.at[pl.ds(0, NX - 1)], crecv.at[1])
    got = cy[0]
    for d in range(1, NX):
        got = got + cx[mod(x + d, NX)]
    cy[1] = got
    me = y * NC + c
    for to in dps:
        copies.send(cy.at[1], cd.at[me], crecv.at[2], to)

    def relay(row, df):
        for k, ds in ((0, -1), (1, 1)):
            wait_recv(spot(df, ds), srecv.at[row, k])
            copies.send(spot(df, ds, k), spot(df, ds, k), srecv.at[row, 2 + k], second_to(-ds))
            copies.send(spot(df, ds), spot(df, ds), sibrecv, sibling)

    relay(0, 0)
    for k in (0, 1):
        wait_recv(spot(2, 0, k), frecv.at[2 + k])
    for d, j in ((1, 0), (-1, 1)):
        copies.send(spot(2, 0), spot(2, 0), srecv.at[3, j], second_to(d))
    copies.send(spot(2, 0), spot(2, 0), sibrecv, sibling)
    relay(1, -1)
    relay(2, 1)
    relay(3, 2)
    for row, df in ((0, 0), (1, -1), (2, 1), (3, 2)):
        for k in (0, 1):
            wait_recv(spot(df, 2, k), srecv.at[row, 2 + k])
        copies.send(spot(df, 2), spot(df, 2), sibrecv, sibling)
    wait_recv(cd.at[pl.ds(0, NY * NC - 1)], crecv.at[2])
    got = cy[1]
    for d in range(1, NY * NC):
        got = got + cd[mod(me + d, NY * NC)]
    total[...] = got
    spot_own.wait()
    other = full.at[:, :, pl.ds(pl.multiple_of((1 - c) * HALF, HALF), HALF)]
    wait_recv(other, sibrecv)
    copies.drain()


def gather(wq, wk, wv, wo, cnt):
    vm = pl.BlockSpec(memory_space=pltpu.VMEM)
    hbm = pl.BlockSpec(memory_space=pl.ANY)
    dma = pltpu.SemaphoreType.DMA
    return pl.pallas_call(
        gather_kernel,
        name="gather_weights",
        out_shape=(jax.ShapeDtypeStruct((4, D, D), BF), jax.ShapeDtypeStruct((1, 128), F32)),
        in_specs=[hbm] * 4 + [vm],
        out_specs=(vm, vm),
        scratch_shapes=[
            pltpu.VMEM((4, SHARD, D), BF),
            pltpu.VMEM((NZ, SHARD, HALF), BF),
            pltpu.VMEM((NZ, 1, 128), F32),
            pltpu.VMEM((NX, 1, 128), F32),
            pltpu.VMEM((NY * NC, 1, 128), F32),
            pltpu.VMEM((2, 1, 128), F32),
            pltpu.VMEM((SLAB, HALF), F32),
            pltpu.VMEM((SLAB, HALF), BF),
            dma((4,)), dma, dma((3,)), dma((4,)), dma((4, 4)), dma, dma((96,)),
        ],
        compiler_params=pltpu.CompilerParams(collective_id=0, has_side_effects=True),
    )(wq, wk, wv, wo, cnt)


def reduce_kernel(part, scale, out, ra, rb, rc, rd, re, rf, ta, tb, tf, tz, rz, own, oz,
                  xrecv, zrecv, orecv, arecv, send_sems):
    x, y, z, c = place()
    zs = [device(x, y, mod(z + d, NZ), c) for d in range(1, NZ)]
    right, left = device(mod(x + 1, NX), y, z, c), device(mod(x - 1, NX), y, z, c)
    xr, xl, xo = mod(x + 1, NX), mod(x - 1, NX), mod(x + 2, NX)
    greet(zs + [right, left])
    copies = Copies(send_sems)
    low, high = pl.ds(0, HPX), pl.ds(HPX, HPX)
    copies.send(part.at[xo, low], ra, xrecv.at[0], right)
    copies.send(part.at[xo, high], rb, xrecv.at[1], left)
    copies.send(part.at[xr, high], rc, xrecv.at[2], right)
    copies.send(part.at[xl, low], rd, xrecv.at[3], left)
    wait_recv(ra, xrecv.at[0])
    ta[...] = (part[xr, 0:HPX].astype(F32) + ra[...].astype(F32)).astype(BF)
    copies.send(ta, re, xrecv.at[4], right)
    wait_recv(rb, xrecv.at[1])
    tb[...] = (part[xl, HPX:2 * HPX].astype(F32) + rb[...].astype(F32)).astype(BF)
    copies.send(tb, rf, xrecv.at[5], left)
    wait_recv(rc, xrecv.at[2])
    wait_recv(rd, xrecv.at[3])
    wait_recv(re, xrecv.at[4])
    wait_recv(rf, xrecv.at[5])
    for h in range(HPX):
        low_sum = part[x, h].astype(F32) + rd[h].astype(F32) + re[h].astype(F32)
        high_sum = part[x, HPX + h].astype(F32) + rc[h].astype(F32) + rf[h].astype(F32)
        tf[:, IPZ * h:IPZ * (h + 1), :] = low_sum.reshape(NZ, IPZ, COLS)
        tf[:, IPZ * (HPX + h):IPZ * (HPX + h + 1), :] = high_sum.reshape(NZ, IPZ, COLS)
    tz[...] = tf[...].astype(BF)
    far = sorted(range(1, NZ), key=lambda d: -min(d, NZ - d))
    for d in far:
        copies.send(tz.at[mod(z + d, NZ)], rz.at[z], zrecv, zs[d - 1])
    wait_recv(rz.at[pl.ds(0, NZ - 1)], zrecv)
    acc = tf[z]
    for d in range(1, NZ):
        acc = acc + rz[mod(z + d, NZ)].astype(F32)
    half = HPX * IPZ
    s = scale[...]
    logits = acc[0:half] * s
    grads = acc[half:2 * half]
    top = jnp.max(logits, axis=-1, keepdims=True)
    expo = jnp.exp(logits - top)
    probs = expo / jnp.sum(expo, axis=-1, keepdims=True)
    glog = probs * (grads - jnp.sum(probs * grads, axis=-1, keepdims=True)) * s
    own[...] = jnp.concatenate([probs, glog], axis=0).astype(BF)
    for d in far:
        copies.send(own, oz.at[z], orecv, zs[d - 1])
    keep = pltpu.make_async_copy(own, oz.at[z], arecv.at[4])
    keep.start()
    keep.wait()
    wait_recv(oz.at[pl.ds(0, NZ - 1)], orecv)
    got = oz[...].astype(F32)
    for k in range(2 * HPX):
        out[x, k] = got[:, IPZ * k:IPZ * (k + 1), :].reshape(COLS, COLS).astype(BF)
    copies.send(out.at[x], out.at[x], arecv.at[0], right)
    copies.send(out.at[x], out.at[x], arecv.at[1], left)
    wait_recv(out.at[xl], arecv.at[0])
    copies.send(out.at[xl, low], out.at[xl, low], arecv.at[2], right)
    wait_recv(out.at[xr], arecv.at[1])
    copies.send(out.at[xr, high], out.at[xr, high], arecv.at[3], left)
    wait_recv(out.at[xo, low], arecv.at[2])
    wait_recv(out.at[xo, high], arecv.at[3])
    copies.drain()


def reduce_scatter_gather(part, scale):
    vm = pl.BlockSpec(memory_space=pltpu.VMEM)
    dma = pltpu.SemaphoreType.DMA
    quarter = pltpu.VMEM((HPX, COLS, COLS), BF)
    return pl.pallas_call(
        reduce_kernel,
        name="reduce_probs",
        out_shape=jax.ShapeDtypeStruct((NX, 2 * HPX, COLS, COLS), BF),
        in_specs=[vm, vm],
        out_specs=vm,
        scratch_shapes=[quarter] * 8 + [
            pltpu.VMEM((NZ, CHUNK, COLS), F32),
            pltpu.VMEM((NZ, CHUNK, COLS), BF),
            pltpu.VMEM((NZ, CHUNK, COLS), BF),
            pltpu.VMEM((CHUNK, COLS), BF),
            pltpu.VMEM((NZ, CHUNK, COLS), BF),
            dma((6,)), dma, dma, dma((5,)), dma((48,)),
        ],
        compiler_params=pltpu.CompilerParams(collective_id=1, has_side_effects=True),
    )(part, scale)


def nt(a, b):
    return lax.dot_general(a, b, (((1,), (1,)), ((), ())), preferred_element_type=F32)


def tn(a, b):
    return lax.dot_general(a, b, (((0,), (0,)), ((), ())), preferred_element_type=F32)


def nn(a, b):
    return lax.dot_general(a, b, (((1,), (0,)), ((), ())), preferred_element_type=F32)


def columns_of(masked):
    out = []
    for r in range(2):
        wide = jnp.broadcast_to(masked[r:r + 1, :], (COLS, COLS))
        out.append(jnp.transpose(wide)[:, 0:1])
    return jnp.concatenate(out, axis=0)


def normalize(hidden):
    widened = hidden.astype(F32)
    average = jnp.mean(widened, axis=-1, keepdims=True)
    centred = widened - average
    variance = jnp.mean(centred * centred, axis=-1, keepdims=True)
    inv_std = lax.rsqrt(variance + EPS)
    return widened, centred * inv_std, inv_std


def by_row(alive):
    rows = lax.broadcasted_iota(jnp.int32, (2 * COLS, 1), 0)
    return jnp.where(rows < COLS, alive[0], alive[1])


def lane_low(shape):
    lane = lax.broadcasted_iota(jnp.int32, shape, len(shape) - 1)
    return lax.rem(lane, 2 * HEAD) < HEAD


HEAD = D // HEADS
PAIR = 2 * HEAD


def side(ref, p):
    return jnp.concatenate(
        [ref[0:COLS, PAIR * p:PAIR * (p + 1)], ref[COLS:2 * COLS, PAIR * p:PAIR * (p + 1)]], axis=1)


def stacked(ref, p, low):
    both = side(ref, p)
    zero = jnp.zeros_like(both)
    return jnp.concatenate([jnp.where(low, both, zero), jnp.where(low, zero, both)], axis=0)


def before_kernel(alive, hidden, masked, cot, gain, full, part, q, k, v, ga):
    widened, x_hat, inv_std = normalize(hidden[...])
    normed = (x_hat * gain[...]).astype(BF)
    live = by_row(alive)
    q[...] = (nn(normed, full[0]).astype(BF).astype(F32) * live).astype(BF)
    k[...] = nn(normed, full[1]).astype(BF)
    v[...] = nn(normed, full[2]).astype(BF)
    weight = columns_of(masked[...].astype(F32)) * live
    gm = (cot[...].astype(F32) * weight).astype(BF)
    ga[...] = nt(gm, full[3]).astype(BF)
    low = lane_low((COLS, 2 * PAIR))
    for p in range(HEADS // 2):
        for base, left, right in ((0, q, k), (HPX, ga, v)):
            both = nt(stacked(left, p, low), side(right, p)).astype(BF)
            for j in range(2):
                h = 2 * p + j
                part[h // HPX, base + h % HPX] = both[COLS * j:COLS * (j + 1)]


def before(alive, hidden, masked, cot, gain, full):
    vm = pl.BlockSpec(memory_space=pltpu.VMEM)
    tokens = jax.ShapeDtypeStruct((2 * COLS, D), BF)
    return pl.pallas_call(
        before_kernel,
        name="before",
        out_shape=(jax.ShapeDtypeStruct((NX, 2 * HPX, COLS, COLS), BF), tokens, tokens, tokens, tokens),
        in_specs=[pl.BlockSpec(memory_space=pltpu.SMEM)] + [vm] * 5,
        out_specs=(vm,) * 5,
    )(alive, hidden, masked, cot, gain, full)


def after_kernel(alive, hidden, masked, cot, gain, full, total, soft, q, k, v, ga, mixed, grad,
                 att, gq, gk, gv):
    live = by_row(alive)
    low = lane_low((COLS, 2 * PAIR))
    for p in range(HEADS // 2):
        h0, h1 = 2 * p, 2 * p + 1
        p0, p1 = soft[h0 // HPX, h0 % HPX], soft[h1 // HPX, h1 % HPX]
        g0, g1 = soft[h0 // HPX, HPX + h0 % HPX], soft[h1 // HPX, HPX + h1 % HPX]
        p_side, p_stack = jnp.concatenate([p0, p1], axis=1), jnp.concatenate([p0, p1], axis=0)
        g_side, g_stack = jnp.concatenate([g0, g1], axis=1), jnp.concatenate([g0, g1], axis=0)
        for dst, value in ((att, nn(p_side, stacked(v, p, low))), (gv, tn(p_stack, stacked(ga, p, low))),
                           (gq, nn(g_side, stacked(k, p, low))), (gk, tn(g_stack, stacked(q, p, low)))):
            value = value.astype(BF)
            dst[0:COLS, PAIR * p:PAIR * (p + 1)] = value[:, 0:PAIR]
            dst[COLS:2 * COLS, PAIR * p:PAIR * (p + 1)] = value[:, PAIR:2 * PAIR]
    widened, x_hat, inv_std = normalize(hidden[...])
    mixed[...] = (widened + live * nn(att[...], full[3])).astype(BF)
    gn = nt(gq[...], full[0]) * live + nt(gk[...], full[1]) + nt(gv[...], full[2])
    scaled = gn * gain[...]
    grad_x = inv_std * (scaled - jnp.mean(scaled, axis=-1, keepdims=True)
                        - x_hat * jnp.mean(scaled * x_hat, axis=-1, keepdims=True))
    ratio = total[0:1, 1:2] * COLS / jnp.maximum(total[0:1, 0:1], 1.0)
    weight = columns_of(masked[...].astype(F32)) * live
    grad[...] = (ratio * (cot[...].astype(F32) * weight + grad_x)).astype(BF)


def after(alive, hidden, masked, cot, gain, full, total, soft, q, k, v, ga):
    vm = pl.BlockSpec(memory_space=pltpu.VMEM)
    tokens = jax.ShapeDtypeStruct((2 * COLS, D), BF)
    return pl.pallas_call(
        after_kernel,
        name="after",
        out_shape=(tokens, tokens),
        in_specs=[pl.BlockSpec(memory_space=pltpu.SMEM)] + [vm] * 11,
        out_specs=(vm, vm),
        scratch_shapes=[pltpu.VMEM((2 * COLS, D), BF)] * 4,
    )(alive, hidden, masked, cot, gain, full, total, soft, q, k, v, ga)


def body(hidden, masked, depths, norm_gain, w_query, w_key, w_value, w_out, cotangent):
    shape = hidden.shape
    first_row = lax.axis_index("row") * shape[1]
    alive = (first_row + jnp.arange(2, dtype=jnp.int32) < depths[0]).astype(F32)
    masks = masked[0]
    counted = jnp.sum(masks.astype(F32) * alive[:, None])
    lane = jnp.arange(128)
    cnt = jnp.where(lane == 0, counted, jnp.where(lane == 1, jnp.sum(alive), 0.0)).reshape(1, 128)
    scale = jnp.broadcast_to(1.0 / jnp.sqrt(depths[0].astype(F32) * HEAD), (1, 128))
    tokens = (shape[1] * shape[2], shape[3])
    hid, cot = hidden.reshape(tokens), cotangent.reshape(tokens)
    gain = norm_gain.reshape(1, D)
    full, total = gather(w_query, w_key, w_value, w_out, cnt)
    part, q, k, v, ga = before(alive, hid, masks, cot, gain, full)
    soft = reduce_scatter_gather(part, scale)
    mixed, grad = after(alive, hid, masks, cot, gain, full, total, soft, q, k, v, ga)
    return mixed.reshape(shape), grad.reshape(shape)


def solution(mesh):
    return jax.shard_map(
        body,
        mesh=mesh,
        in_specs=(
            P("dp", "row", None, None),
            P("dp", "row", None),
            P("dp"),
            P(),
            P("row", None),
            P("row", None),
            P("row", None),
            P("row", None),
            P("dp", "row", None, None),
        ),
        out_specs=(P("dp", "row", None, None), P("dp", "row", None, None)),
        check_vma=False,
    )
```

```python
import jax
import jax.numpy as jnp
from jax import lax
from jax.experimental import pallas as pl
from jax.experimental.pallas import tpu as pltpu
from jax.sharding import PartitionSpec as P

HEADS = 12
EPS = 1e-05
NX, NY, NZ, NC = 4, 4, 16, 2
D = 768
COLS = 128
SHARD = D // (NX * NZ)
SLAB = SHARD * NZ
HALF = D // NC
HPX = HEADS // NX
IPZ = COLS // NZ
CHUNK = HPX * IPZ
HEAD = D // HEADS
PAIR = 2 * HEAD
MESH = pl.DeviceIdType.MESH
BF, F32 = jnp.bfloat16, jnp.float32


def place():
    dp, row = lax.axis_index("dp"), lax.axis_index("row")
    return lax.div(row, NZ), lax.div(dp, NC), lax.rem(row, NZ), lax.rem(dp, NC)


def device(x, y, z, c):
    return (y * NC + c, x * NZ + z)


def mod(a, n):
    return lax.rem(a + n, n)


class Copies:
    def __init__(self, sems, group_sems):
        self.sems, self.sent = sems, []
        self.group_sems, self.groups = group_sems, []

    def spread(self, sources, dst, recv, devices, all_of):
        sem = self.group_sems.at[len(self.groups)]
        for src, to in zip(sources, devices, strict=True):
            pltpu.make_async_remote_copy(
                src_ref=src, dst_ref=dst, send_sem=sem, recv_sem=recv, device_id=to, device_id_type=MESH).start()
        self.groups.append((all_of, sem))

    def send(self, src, dst, recv, to):
        copy = pltpu.make_async_remote_copy(
            src_ref=src, dst_ref=dst, send_sem=self.sems.at[len(self.sent)], recv_sem=recv,
            device_id=to, device_id_type=MESH)
        copy.start()
        self.sent.append(copy)

    def drain(self):
        for copy in self.sent:
            copy.wait_send()
        for ref, sem in self.groups:
            wait_recv(ref, sem)


def wait_recv(ref, sem):
    pltpu.make_async_copy(ref, ref, sem).wait()


def nt(a, b):
    return lax.dot_general(a, b, (((1,), (1,)), ((), ())), preferred_element_type=F32)


def tn(a, b):
    return lax.dot_general(a, b, (((0,), (0,)), ((), ())), preferred_element_type=F32)


def nn(a, b):
    return lax.dot_general(a, b, (((1,), (0,)), ((), ())), preferred_element_type=F32)


def columns_of(masked):
    out = []
    for r in range(2):
        wide = jnp.broadcast_to(masked[r:r + 1, :], (COLS, COLS))
        out.append(jnp.transpose(wide)[:, 0:1])
    return jnp.concatenate(out, axis=0)


def lane_low(shape):
    lane = lax.broadcasted_iota(jnp.int32, shape, len(shape) - 1)
    return lax.rem(lane, 2 * HEAD) < HEAD


def side(ref, p):
    return jnp.concatenate(
        [ref[0:COLS, PAIR * p:PAIR * (p + 1)], ref[COLS:2 * COLS, PAIR * p:PAIR * (p + 1)]], axis=1)


def stacked(ref, p, low):
    both = side(ref, p)
    zero = jnp.zeros_like(both)
    return jnp.concatenate([jnp.where(low, both, zero), jnp.where(low, zero, both)], axis=0)


def step_kernel(depth, hidden, masked, gain, wq, wk, wv, wo, cot, mixed, grad,
                full, stack, zbuf, cz, cx, cd, cy, tmp, blk, x_hat, inv_std, normed, gm, weight, live,
                q, k, v, ga, att, gq, gk, gv, part, ra, rb, rd, rc, re, rf, ta, tb, tf, tz, rz, own, oz, soft,
                local, zrecv, crecv, frecv, srecv, sibrecv, xrecv, rrecv, orecv, arecv, send_sems, group_sems):
    x, y, z, c = place()
    loads = [pltpu.make_async_copy(w, stack.at[i], local.at[i]) for i, w in enumerate((wq, wk, wv, wo))]
    for load in loads:
        load.start()
    far = sorted(range(1, NZ), key=lambda d: -min(d, NZ - d))
    zs = [device(x, y, mod(z + d, NZ), c) for d in far]
    xs = [device(mod(x + d, NX), y, z, c) for d in range(1, NX)]
    dps = [device(x, lax.div(e, NC), z, lax.rem(e, NC))
           for e in [mod(y * NC + c + d, NY * NC) for d in range(1, NY * NC)]]
    right, left = xs[0], xs[NX - 2]
    barrier = pltpu.get_barrier_semaphore()
    for to in zs + xs + dps:
        pl.semaphore_signal(barrier, inc=1, device_id=to, device_id_type=MESH)

    widened = hidden[...].astype(F32)
    centred = widened - jnp.mean(widened, axis=-1, keepdims=True)
    inv = lax.rsqrt(jnp.mean(centred * centred, axis=-1, keepdims=True) + EPS)
    inv_std[...] = inv
    x_hat[...] = centred * inv
    normed[...] = (centred * inv * gain[...].reshape(1, D)).astype(BF)
    rows = lax.broadcasted_iota(jnp.int32, (2 * COLS, 1), 0)
    alive = ((x * NZ + z) * 2 + lax.div(rows, COLS) < depth[0]).astype(F32)
    live[...] = alive
    token = columns_of(masked[...].astype(F32)) * alive
    weight[...] = token
    gm[...] = (cot[...].astype(F32) * token).astype(BF)
    lane = lax.broadcasted_iota(jnp.int32, (1, 128), 1)
    counted = jnp.sum(token, axis=0, keepdims=True)
    rows_live = jnp.sum(alive, axis=0, keepdims=True)
    cy[2] = jnp.where(lane == 0, counted, jnp.where(lane == 1, rows_live, 0.0))

    for load in loads:
        load.wait()
    pl.semaphore_wait(barrier, NZ - 1 + NX - 1 + NY * NC - 1)

    copies = Copies(send_sems, group_sems)
    mine = stack.at[y, :, pl.ds(pl.multiple_of(c * HALF, HALF), HALF)]
    others = pl.ds(0, NZ - 1)
    copies.spread([mine] * (NZ - 1), zbuf.at[z], zrecv, zs, zbuf.at[others])
    copies.spread([cy.at[2]] * (NZ - 1), cz.at[z], crecv.at[0], zs, cz.at[others])
    keep = pltpu.make_async_copy(mine, zbuf.at[z], local.at[0])
    keep.start()
    keep.wait()
    cz[z] = cy[2]
    wait_recv(zbuf.at[others], zrecv)
    for i in range(NZ):
        tmp[SHARD * i:SHARD * (i + 1), :] = zbuf[i].astype(F32)
    blk[...] = tmp[...].astype(BF)

    def spot(df, ds, piece=None):
        bx = mod(x + df * (1 - c) + ds * c, NX)
        by = mod(y + df * c + ds * (1 - c), NY)
        first, count = (0, SLAB) if piece is None else (piece * (SLAB // 2), SLAB // 2)
        return full.at[by, pl.ds(pl.multiple_of(bx * SLAB + first, 16), count),
                       pl.ds(pl.multiple_of(c * HALF, HALF), HALF)]

    def first_to(d):
        return device(mod(x + d * (1 - c), NX), mod(y + d * c, NY), z, c)

    def second_to(d):
        return device(mod(x + d * c, NX), mod(y + d * (1 - c), NY), z, c)

    sibling = device(x, y, z, 1 - c)
    spot_own = pltpu.make_async_copy(blk, spot(0, 0), local.at[0])
    spot_own.start()
    for d, j in ((1, 0), (-1, 1)):
        copies.send(blk, spot(0, 0), frecv.at[j], first_to(d))
    for d, j in ((1, 0), (-1, 1)):
        copies.send(blk, spot(0, 0), srecv.at[0, j], second_to(d))
    copies.send(blk, spot(0, 0), sibrecv, sibling)

    wait_recv(cz.at[others], crecv.at[0])
    cy[0] = jnp.sum(cz[...], axis=0)
    for to in xs:
        copies.send(cy.at[0], cx.at[x], crecv.at[1], to)

    for i, df in ((0, -1), (1, 1)):
        wait_recv(spot(df, 0), frecv.at[i])
        copies.send(spot(df, 0, i), spot(df, 0, i), frecv.at[2 + i], first_to(-df))
        for d, j in ((1, 0), (-1, 1)):
            copies.send(spot(df, 0), spot(df, 0), srecv.at[1 + i, j], second_to(d))
        copies.send(spot(df, 0), spot(df, 0), sibrecv, sibling)

    wait_recv(cx.at[pl.ds(0, NX - 1)], crecv.at[1])
    got = cy[0]
    for d in range(1, NX):
        got = got + cx[mod(x + d, NX)]
    cy[1] = got
    me = y * NC + c
    for to in dps:
        copies.send(cy.at[1], cd.at[me], crecv.at[2], to)

    def relay(row, df):
        for i, ds in ((0, -1), (1, 1)):
            wait_recv(spot(df, ds), srecv.at[row, i])
            copies.send(spot(df, ds, i), spot(df, ds, i), srecv.at[row, 2 + i], second_to(-ds))
            copies.send(spot(df, ds), spot(df, ds), sibrecv, sibling)

    relay(0, 0)
    for i in (0, 1):
        wait_recv(spot(2, 0, i), frecv.at[2 + i])
    for d, j in ((1, 0), (-1, 1)):
        copies.send(spot(2, 0), spot(2, 0), srecv.at[3, j], second_to(d))
    copies.send(spot(2, 0), spot(2, 0), sibrecv, sibling)
    relay(1, -1)
    relay(2, 1)
    relay(3, 2)
    for row, df in ((0, 0), (1, -1), (2, 1), (3, 2)):
        for i in (0, 1):
            wait_recv(spot(df, 2, i), srecv.at[row, 2 + i])
        copies.send(spot(df, 2), spot(df, 2), sibrecv, sibling)
    spot_own.wait()
    wait_recv(full.at[:, :, pl.ds(pl.multiple_of((1 - c) * HALF, HALF), HALF)], sibrecv)

    xr, xl, xo = mod(x + 1, NX), mod(x - 1, NX), mod(x + 2, NX)
    low = lane_low((COLS, 2 * PAIR))
    logit, slope = 0, 1

    def partial(side_of, with_, kind):
        for p in range(HEADS // 2):
            both = nt(stacked(side_of, p, low), side(with_, p)).astype(BF)
            for j in range(2):
                h = 2 * p + j
                part[kind, h // HPX, h % HPX] = both[COLS * j:COLS * (j + 1)]

    q[...] = (nn(normed[...], full[0]).astype(BF).astype(F32) * live[...]).astype(BF)
    k[...] = nn(normed[...], full[1]).astype(BF)
    partial(q, k, logit)
    copies.send(part.at[logit, xo], ra, xrecv.at[0], right)
    copies.send(part.at[logit, xl], rd, xrecv.at[3], left)
    v[...] = nn(normed[...], full[2]).astype(BF)
    ga[...] = nt(gm[...], full[3]).astype(BF)
    partial(ga, v, slope)
    copies.send(part.at[slope, xo], rb, xrecv.at[1], left)
    copies.send(part.at[slope, xr], rc, xrecv.at[2], right)
    wait_recv(ra, xrecv.at[0])
    ta[...] = (part[logit, xr].astype(F32) + ra[...].astype(F32)).astype(BF)
    copies.send(ta, re, xrecv.at[4], right)
    wait_recv(rb, xrecv.at[1])
    tb[...] = (part[slope, xl].astype(F32) + rb[...].astype(F32)).astype(BF)
    copies.send(tb, rf, xrecv.at[5], left)

    for kind, one, sem_one, two, sem_two in ((logit, rd, 3, re, 4), (slope, rc, 2, rf, 5)):
        wait_recv(one, xrecv.at[sem_one])
        wait_recv(two, xrecv.at[sem_two])
        for h in range(HPX):
            value = part[kind, x, h].astype(F32) + one[h].astype(F32) + two[h].astype(F32)
            tf[kind, :, IPZ * h:IPZ * (h + 1), :] = value.reshape(NZ, IPZ, COLS)
        tz[kind] = tf[kind].astype(BF)
        copies.spread([tz.at[kind, mod(z + d, NZ)] for d in far], rz.at[kind, z], rrecv.at[kind], zs,
                      rz.at[kind, others])

    def over_z(kind):
        wait_recv(rz.at[kind, others], rrecv.at[kind])
        acc = tf[kind, z]
        for d in range(1, NZ):
            acc = acc + rz[kind, mod(z + d, NZ)].astype(F32)
        return acc

    def spread_rows(kind, value):
        own[kind] = value.astype(BF)
        copies.spread([own.at[kind]] * (NZ - 1), oz.at[kind, z], orecv.at[kind], zs, oz.at[kind, others])
        oz[kind, z] = value.astype(BF)

    scale = 1.0 / jnp.sqrt(jnp.full((1, COLS), depth[0], jnp.int32).astype(F32) * HEAD)
    logits = over_z(logit) * scale
    expo = jnp.exp(logits - jnp.max(logits, axis=-1, keepdims=True))
    probs = expo / jnp.sum(expo, axis=-1, keepdims=True)
    spread_rows(logit, probs)
    slopes = over_z(slope)
    spread_rows(slope, probs * (slopes - jnp.sum(probs * slopes, axis=-1, keepdims=True)) * scale)

    for kind in (logit, slope):
        wait_recv(oz.at[kind, others], orecv.at[kind])
        got = oz[kind].astype(F32)
        for h in range(HPX):
            soft[kind, x, h] = got[:, IPZ * h:IPZ * (h + 1), :].reshape(COLS, COLS).astype(BF)
        ahead, behind = (right, left) if kind == logit else (left, right)
        copies.send(soft.at[kind, x], soft.at[kind, x], arecv.at[kind, 0], ahead)
        copies.send(soft.at[kind, x], soft.at[kind, x], arecv.at[kind, 1], behind)

    def collect(kind):
        near = xl if kind == logit else xr
        wait_recv(soft.at[kind, near], arecv.at[kind, 0])
        copies.send(soft.at[kind, near], soft.at[kind, near], arecv.at[kind, 2], right if kind == logit else left)

    def finish(kind):
        wait_recv(soft.at[kind, xr if kind == logit else xl], arecv.at[kind, 1])
        wait_recv(soft.at[kind, xo], arecv.at[kind, 2])

    def apply(kind, across, across_to, down, down_to):
        for p in range(HEADS // 2):
            h0, h1 = 2 * p, 2 * p + 1
            s0, s1 = soft[kind, h0 // HPX, h0 % HPX], soft[kind, h1 // HPX, h1 % HPX]
            for dst, value in (
                    (across_to, nn(jnp.concatenate([s0, s1], axis=1), stacked(across, p, low))),
                    (down_to, tn(jnp.concatenate([s0, s1], axis=0), stacked(down, p, low)))):
                value = value.astype(BF)
                dst[0:COLS, PAIR * p:PAIR * (p + 1)] = value[:, 0:PAIR]
                dst[COLS:2 * COLS, PAIR * p:PAIR * (p + 1)] = value[:, PAIR:2 * PAIR]

    collect(logit)
    collect(slope)
    finish(logit)
    apply(logit, v, att, ga, gv)
    mixed[...] = (hidden[...].astype(F32) + live[...] * nn(att[...], full[3])).astype(BF)
    acc = nt(gv[...], full[2])
    finish(slope)
    apply(slope, k, gq, q, gk)
    acc = acc + nt(gq[...], full[0]) * live[...] + nt(gk[...], full[1])
    scaled = acc * gain[...].reshape(1, D)
    hat = x_hat[...]
    grad_x = inv_std[...] * (scaled - jnp.mean(scaled, axis=-1, keepdims=True)
                             - hat * jnp.mean(scaled * hat, axis=-1, keepdims=True))
    wait_recv(cd.at[pl.ds(0, NY * NC - 1)], crecv.at[2])
    total = cy[1]
    for d in range(1, NY * NC):
        total = total + cd[mod(me + d, NY * NC)]
    ratio = total[:, 1:2] / jnp.maximum(total[:, 0:1], 1.0)
    grad[...] = (ratio * (cot[...].astype(F32) * weight[...] + grad_x)).astype(BF)
    copies.drain()


def step(depths, hidden, masked, gain, wq, wk, wv, wo, cot):
    vm = pl.BlockSpec(memory_space=pltpu.VMEM)
    hbm = pl.BlockSpec(memory_space=pl.ANY)
    dma = pltpu.SemaphoreType.DMA
    tokens = jax.ShapeDtypeStruct((2 * COLS, D), BF)
    act, col = pltpu.VMEM((2 * COLS, D), BF), pltpu.VMEM((2 * COLS, 1), F32)
    quarter = pltpu.VMEM((HPX, COLS, COLS), BF)
    chunks = pltpu.VMEM((2, NZ, CHUNK, COLS), BF)
    heads = pltpu.VMEM((2, NX, HPX, COLS, COLS), BF)
    return pl.pallas_call(
        step_kernel,
        name="step",
        out_shape=(tokens, tokens),
        in_specs=[pl.BlockSpec(memory_space=pltpu.SMEM), vm, vm, vm] + [hbm] * 4 + [vm],
        out_specs=(vm, vm),
        scratch_shapes=[
            pltpu.VMEM((4, D, D), BF),
            pltpu.VMEM((4, SHARD, D), BF),
            pltpu.VMEM((NZ, SHARD, HALF), BF),
            pltpu.VMEM((NZ, 1, 128), F32),
            pltpu.VMEM((NX, 1, 128), F32),
            pltpu.VMEM((NY * NC, 1, 128), F32),
            pltpu.VMEM((3, 1, 128), F32),
            pltpu.VMEM((SLAB, HALF), F32),
            pltpu.VMEM((SLAB, HALF), BF),
            pltpu.VMEM((2 * COLS, D), F32), col, act, act, col, col,
            act, act, act, act, act, act, act, act,
            heads, quarter, quarter, quarter, quarter, quarter, quarter, quarter, quarter,
            pltpu.VMEM((2, NZ, CHUNK, COLS), F32), chunks, chunks, pltpu.VMEM((2, CHUNK, COLS), BF), chunks, heads,
            dma((4,)), dma, dma((3,)), dma((4,)), dma((4, 4)), dma, dma((6,)), dma((2,)), dma((2,)), dma((2, 3)),
            dma((80,)), dma((6,)),
        ],
        compiler_params=pltpu.CompilerParams(collective_id=0, has_side_effects=True),
    )(depths, hidden, masked, gain, wq, wk, wv, wo, cot)


def body(hidden, masked, depths, norm_gain, w_query, w_key, w_value, w_out, cotangent):
    shape = hidden.shape
    tokens = (shape[1] * shape[2], shape[3])
    mixed, grad = step(depths, hidden.reshape(tokens), masked[0], norm_gain, w_query, w_key, w_value, w_out,
                       cotangent.reshape(tokens))
    return mixed.reshape(shape), grad.reshape(shape)


def solution(mesh):
    return jax.shard_map(
        body,
        mesh=mesh,
        in_specs=(
            P("dp", "row", None, None),
            P("dp", "row", None),
            P("dp"),
            P(),
            P("row", None),
            P("row", None),
            P("row", None),
            P("row", None),
            P("dp", "row", None, None),
        ),
        out_specs=(P("dp", "row", None, None), P("dp", "row", None, None)),
        check_vma=False,
    )
```

```python
import jax
import jax.numpy as jnp
from jax import lax
from jax.experimental import pallas as pl
from jax.experimental.pallas import tpu as pltpu
from jax.sharding import PartitionSpec as P

HEADS = 12
EPS = 1e-05
NX, NY, NZ, NC = 4, 4, 16, 2
D = 768
COLS = 128
SHARD = D // (NX * NZ)
SLAB = SHARD * NZ
HALF = D // NC
HPX = HEADS // NX
IPZ = COLS // NZ
CHUNK = HPX * IPZ
HEAD = D // HEADS
PAIR = 2 * HEAD
MESH = pl.DeviceIdType.MESH
BF, F32 = jnp.bfloat16, jnp.float32


def place():
    dp, row = lax.axis_index("dp"), lax.axis_index("row")
    return lax.div(row, NZ), lax.div(dp, NC), lax.rem(row, NZ), lax.rem(dp, NC)


def device(x, y, z, c):
    return (y * NC + c, x * NZ + z)


def mod(a, n):
    return lax.rem(a + n, n)


class Copies:
    def __init__(self, sems, group_sems):
        self.sems, self.sent = sems, []
        self.group_sems, self.groups = group_sems, []

    def spread(self, sources, dst, recv, devices, all_of):
        sem = self.group_sems.at[len(self.groups)]
        for src, to in zip(sources, devices, strict=True):
            pltpu.make_async_remote_copy(
                src_ref=src, dst_ref=dst, send_sem=sem, recv_sem=recv, device_id=to, device_id_type=MESH).start()
        self.groups.append((all_of, sem))

    def send(self, src, dst, recv, to):
        copy = pltpu.make_async_remote_copy(
            src_ref=src, dst_ref=dst, send_sem=self.sems.at[len(self.sent)], recv_sem=recv,
            device_id=to, device_id_type=MESH)
        copy.start()
        self.sent.append(copy)

    def drain(self):
        for copy in self.sent:
            copy.wait_send()
        for ref, sem in self.groups:
            wait_recv(ref, sem)


def wait_recv(ref, sem):
    pltpu.make_async_copy(ref, ref, sem).wait()


def nt(a, b):
    return lax.dot_general(a, b, (((1,), (1,)), ((), ())), preferred_element_type=F32)


def tn(a, b):
    return lax.dot_general(a, b, (((0,), (0,)), ((), ())), preferred_element_type=F32)


def nn(a, b):
    return lax.dot_general(a, b, (((1,), (0,)), ((), ())), preferred_element_type=F32)


def columns_of(masked):
    out = []
    for r in range(2):
        wide = jnp.broadcast_to(masked[r:r + 1, :], (COLS, COLS))
        out.append(jnp.transpose(wide)[:, 0:1])
    return jnp.concatenate(out, axis=0)


def lane_low(shape):
    lane = lax.broadcasted_iota(jnp.int32, shape, len(shape) - 1)
    return lax.rem(lane, 2 * HEAD) < HEAD


def side(ref, p):
    return jnp.concatenate(
        [ref[0:COLS, PAIR * p:PAIR * (p + 1)], ref[COLS:2 * COLS, PAIR * p:PAIR * (p + 1)]], axis=1)


def stacked(ref, p, low):
    both = side(ref, p)
    zero = jnp.zeros_like(both)
    return jnp.concatenate([jnp.where(low, both, zero), jnp.where(low, zero, both)], axis=0)


def step_kernel(depth, hidden, masked, gain, wq, wk, wv, wo, cot, mixed, grad,
                full, stack, zbuf, cz, cx, cd, cy, tmp, blk, x_hat, inv_std, normed, gm, weight, live,
                q, k, v, ga, att, gq, gk, gv, part, rx, tf, tz, rz, own, oz, soft,
                local, zrecv, crecv, frecv, srecv, sibrecv, xrecv, rrecv, orecv, arecv, send_sems, group_sems):
    x, y, z, c = place()
    loads = [pltpu.make_async_copy(w, stack.at[i], local.at[i]) for i, w in enumerate((wq, wk, wv, wo))]
    for load in loads:
        load.start()
    far = sorted(range(1, NZ), key=lambda d: -min(d, NZ - d))
    zs = [device(x, y, mod(z + d, NZ), c) for d in far]
    xs = [device(mod(x + d, NX), y, z, c) for d in (2, 1, 3)]
    dps = [device(x, lax.div(e, NC), z, lax.rem(e, NC))
           for e in [mod(y * NC + c + d, NY * NC) for d in range(1, NY * NC)]]
    def along(d):
        return device(x, y, mod(z + d, NZ), c)

    reach = NZ // 4
    steps = [d * e for d in range(reach, 0, -1) for e in (1, -1)]
    near = [along(d) for d in steps]
    barrier = pltpu.get_barrier_semaphore()
    for to in near + xs + dps:
        pl.semaphore_signal(barrier, inc=1, device_id=to, device_id_type=MESH)

    for load in loads:
        load.wait()
    pl.semaphore_wait(barrier, 2 * reach + NX - 1 + NY * NC - 1)

    copies = Copies(send_sems, group_sems)
    mine = stack.at[y, :, pl.ds(pl.multiple_of(c * HALF, HALF), HALF)]
    others = pl.ds(0, NZ - 1)
    for d, to in zip(steps, near, strict=True):
        copies.send(mine, zbuf.at[z], zrecv.at[0 if abs(d) < reach else 1 if d > 0 else 2], to)
    keep = pltpu.make_async_copy(mine, zbuf.at[z], local.at[0])
    keep.start()
    for sign, sem in ((1, 1), (-1, 2)):
        came = zbuf.at[mod(z - sign * reach, NZ)]
        wait_recv(came, zrecv.at[sem])
        for d in range(reach if sign > 0 else reach - 1, 0, -1):
            copies.send(came, came, zrecv.at[3], along(sign * d))

    widened = hidden[...].astype(F32)
    centred = widened - jnp.mean(widened, axis=-1, keepdims=True)
    inv = lax.rsqrt(jnp.mean(centred * centred, axis=-1, keepdims=True) + EPS)
    inv_std[...] = inv
    x_hat[...] = centred * inv
    normed[...] = (centred * inv * gain[...].reshape(1, D)).astype(BF)
    rows = lax.broadcasted_iota(jnp.int32, (2 * COLS, 1), 0)
    alive = ((x * NZ + z) * 2 + lax.div(rows, COLS) < depth[0]).astype(F32)
    live[...] = alive
    token = columns_of(masked[...].astype(F32)) * alive
    weight[...] = token
    gm[...] = (cot[...].astype(F32) * token).astype(BF)
    lane = lax.broadcasted_iota(jnp.int32, (1, 128), 1)
    counted = jnp.sum(token, axis=0, keepdims=True)
    rows_live = jnp.sum(alive, axis=0, keepdims=True)
    cy[2] = jnp.where(lane == 0, counted, jnp.where(lane == 1, rows_live, 0.0))
    cz[z] = cy[2]
    keep.wait()
    wait_recv(zbuf.at[pl.ds(0, 2 * reach - 2)], zrecv.at[0])
    wait_recv(zbuf.at[pl.ds(0, NZ - 1 - 2 * reach)], zrecv.at[3])
    for i in range(NZ):
        tmp[SHARD * i:SHARD * (i + 1), :] = zbuf[i].astype(F32)
    blk[...] = tmp[...].astype(BF)

    def spot(df, ds, piece=None):
        bx = mod(x + df * (1 - c) + ds * c, NX)
        by = mod(y + df * c + ds * (1 - c), NY)
        first, count = (0, SLAB) if piece is None else (piece * (SLAB // 2), SLAB // 2)
        return full.at[by, pl.ds(pl.multiple_of(bx * SLAB + first, 16), count),
                       pl.ds(pl.multiple_of(c * HALF, HALF), HALF)]

    def first_to(d):
        return device(mod(x + d * (1 - c), NX), mod(y + d * c, NY), z, c)

    def second_to(d):
        return device(mod(x + d * c, NX), mod(y + d * (1 - c), NY), z, c)

    sibling = device(x, y, z, 1 - c)
    spot_own = pltpu.make_async_copy(blk, spot(0, 0), local.at[0])
    spot_own.start()
    for d, j in ((2, 2), (1, 0), (-1, 1)):
        copies.send(blk, spot(0, 0), frecv.at[j], first_to(d))
    for d, j in ((1, 0), (-1, 1)):
        copies.send(blk, spot(0, 0), srecv.at[0, j], second_to(d))
    copies.send(blk, spot(0, 0), sibrecv, sibling)

    copies.spread([cy.at[2]] * (NZ - 1), cz.at[z], crecv.at[0], zs, cz.at[others])
    for i, df in ((0, -1), (1, 1)):
        wait_recv(spot(df, 0), frecv.at[i])
        for d, j in ((1, 0), (-1, 1)):
            copies.send(spot(df, 0), spot(df, 0), srecv.at[1 + i, j], second_to(d))
        copies.send(spot(df, 0), spot(df, 0), sibrecv, sibling)

    def relay(row, df):
        for i, ds in ((0, -1), (1, 1)):
            wait_recv(spot(df, ds), srecv.at[row, i])
            copies.send(spot(df, ds, i), spot(df, ds, i), srecv.at[row, 2 + i], second_to(-ds))
            copies.send(spot(df, ds), spot(df, ds), sibrecv, sibling)

    wait_recv(spot(2, 0), frecv.at[2])
    for d, j in ((2, 2), (1, 0), (-1, 1)):
        copies.send(spot(2, 0), spot(2, 0), srecv.at[3, j], second_to(d))
    copies.send(spot(2, 0), spot(2, 0), sibrecv, sibling)
    relay(0, 0)
    wait_recv(cz.at[others], crecv.at[0])
    cy[0] = jnp.sum(cz[...], axis=0)
    for to in xs:
        copies.send(cy.at[0], cx.at[x], crecv.at[1], to)

    relay(1, -1)
    relay(2, 1)
    wait_recv(cx.at[pl.ds(0, NX - 1)], crecv.at[1])
    got = cy[0]
    for d in range(1, NX):
        got = got + cx[mod(x + d, NX)]
    cy[1] = got
    me = y * NC + c
    for to in dps:
        copies.send(cy.at[1], cd.at[me], crecv.at[2], to)

    for i, ds in ((0, -1), (1, 1)):
        wait_recv(spot(2, ds), srecv.at[3, i])
        copies.send(spot(2, ds), spot(2, ds), sibrecv, sibling)
    for row, df in ((0, 0), (1, -1), (2, 1)):
        for i in (0, 1):
            wait_recv(spot(df, 2, i), srecv.at[row, 2 + i])
        copies.send(spot(df, 2), spot(df, 2), sibrecv, sibling)
    wait_recv(spot(2, 2), srecv.at[3, 2])
    copies.send(spot(2, 2), spot(2, 2), sibrecv, sibling)
    spot_own.wait()
    wait_recv(full.at[:, :, pl.ds(pl.multiple_of((1 - c) * HALF, HALF), HALF)], sibrecv)

    rest = pl.ds(0, NX - 1)
    low = lane_low((COLS, 2 * PAIR))
    logit, slope = 0, 1

    def partial(side_of, with_, kind):
        for p in range(HEADS // 2):
            both = nt(stacked(side_of, p, low), side(with_, p)).astype(BF)
            for j in range(2):
                h = 2 * p + j
                part[kind, h // HPX, h % HPX] = both[COLS * j:COLS * (j + 1)]

    def over_x(kind):
        copies.spread([part.at[kind, mod(x + d, NX)] for d in (2, 1, 3)], rx.at[kind, x], xrecv.at[kind], xs,
                      rx.at[kind, rest])

    q[...] = (nn(normed[...], full[0]).astype(BF).astype(F32) * live[...]).astype(BF)
    k[...] = nn(normed[...], full[1]).astype(BF)
    partial(q, k, logit)
    over_x(logit)
    v[...] = nn(normed[...], full[2]).astype(BF)
    ga[...] = nt(gm[...], full[3]).astype(BF)
    partial(ga, v, slope)
    over_x(slope)

    for kind in (logit, slope):
        wait_recv(rx.at[kind, rest], xrecv.at[kind])
        for h in range(HPX):
            value = part[kind, x, h].astype(F32)
            for d in range(1, NX):
                value = value + rx[kind, mod(x + d, NX), h].astype(F32)
            tf[kind, :, IPZ * h:IPZ * (h + 1), :] = value.reshape(NZ, IPZ, COLS)
        tz[kind] = tf[kind].astype(BF)
        copies.spread([tz.at[kind, mod(z + d, NZ)] for d in far], rz.at[kind, z], rrecv.at[kind], zs,
                      rz.at[kind, others])

    def over_z(kind):
        wait_recv(rz.at[kind, others], rrecv.at[kind])
        acc = tf[kind, z]
        for d in range(1, NZ):
            acc = acc + rz[kind, mod(z + d, NZ)].astype(F32)
        return acc

    def spread_rows(kind, value):
        own[kind] = value.astype(BF)
        copies.spread([own.at[kind]] * (NZ - 1), oz.at[kind, z], orecv.at[kind], zs, oz.at[kind, others])
        oz[kind, z] = value.astype(BF)

    scale = 1.0 / jnp.sqrt(jnp.full((1, COLS), depth[0], jnp.int32).astype(F32) * HEAD)
    logits = over_z(logit) * scale
    expo = jnp.exp(logits - jnp.max(logits, axis=-1, keepdims=True))
    probs = expo / jnp.sum(expo, axis=-1, keepdims=True)
    spread_rows(logit, probs)
    slopes = over_z(slope)
    spread_rows(slope, probs * (slopes - jnp.sum(probs * slopes, axis=-1, keepdims=True)) * scale)

    for kind in (logit, slope):
        wait_recv(oz.at[kind, others], orecv.at[kind])
        got = oz[kind].astype(F32)
        for h in range(HPX):
            soft[kind, x, h] = got[:, IPZ * h:IPZ * (h + 1), :].reshape(COLS, COLS).astype(BF)
        copies.spread([soft.at[kind, x]] * (NX - 1), soft.at[kind, x], arecv.at[kind], xs, soft.at[kind, rest])

    def apply(kind, across, across_to, down, down_to):
        for p in range(HEADS // 2):
            h0, h1 = 2 * p, 2 * p + 1
            s0, s1 = soft[kind, h0 // HPX, h0 % HPX], soft[kind, h1 // HPX, h1 % HPX]
            for dst, value in (
                    (across_to, nn(jnp.concatenate([s0, s1], axis=1), stacked(across, p, low))),
                    (down_to, tn(jnp.concatenate([s0, s1], axis=0), stacked(down, p, low)))):
                value = value.astype(BF)
                dst[0:COLS, PAIR * p:PAIR * (p + 1)] = value[:, 0:PAIR]
                dst[COLS:2 * COLS, PAIR * p:PAIR * (p + 1)] = value[:, PAIR:2 * PAIR]

    wait_recv(soft.at[logit, rest], arecv.at[logit])
    apply(logit, v, att, ga, gv)
    mixed[...] = (hidden[...].astype(F32) + live[...] * nn(att[...], full[3])).astype(BF)
    acc = nt(gv[...], full[2])
    wait_recv(soft.at[slope, rest], arecv.at[slope])
    apply(slope, k, gq, q, gk)
    acc = acc + nt(gq[...], full[0]) * live[...] + nt(gk[...], full[1])
    scaled = acc * gain[...].reshape(1, D)
    hat = x_hat[...]
    grad_x = inv_std[...] * (scaled - jnp.mean(scaled, axis=-1, keepdims=True)
                             - hat * jnp.mean(scaled * hat, axis=-1, keepdims=True))
    wait_recv(cd.at[pl.ds(0, NY * NC - 1)], crecv.at[2])
    total = cy[1]
    for d in range(1, NY * NC):
        total = total + cd[mod(me + d, NY * NC)]
    ratio = total[:, 1:2] / jnp.maximum(total[:, 0:1], 1.0)
    grad[...] = (ratio * (cot[...].astype(F32) * weight[...] + grad_x)).astype(BF)
    copies.drain()


def step(depths, hidden, masked, gain, wq, wk, wv, wo, cot):
    vm = pl.BlockSpec(memory_space=pltpu.VMEM)
    hbm = pl.BlockSpec(memory_space=pl.ANY)
    dma = pltpu.SemaphoreType.DMA
    tokens = jax.ShapeDtypeStruct((2 * COLS, D), BF)
    act, col = pltpu.VMEM((2 * COLS, D), BF), pltpu.VMEM((2 * COLS, 1), F32)
    chunks = pltpu.VMEM((2, NZ, CHUNK, COLS), BF)
    heads = pltpu.VMEM((2, NX, HPX, COLS, COLS), BF)
    return pl.pallas_call(
        step_kernel,
        name="step",
        out_shape=(tokens, tokens),
        in_specs=[pl.BlockSpec(memory_space=pltpu.SMEM), vm, vm, vm] + [hbm] * 4 + [vm],
        out_specs=(vm, vm),
        scratch_shapes=[
            pltpu.VMEM((4, D, D), BF),
            pltpu.VMEM((4, SHARD, D), BF),
            pltpu.VMEM((NZ, SHARD, HALF), BF),
            pltpu.VMEM((NZ, 1, 128), F32),
            pltpu.VMEM((NX, 1, 128), F32),
            pltpu.VMEM((NY * NC, 1, 128), F32),
            pltpu.VMEM((3, 1, 128), F32),
            pltpu.VMEM((SLAB, HALF), F32),
            pltpu.VMEM((SLAB, HALF), BF),
            pltpu.VMEM((2 * COLS, D), F32), col, act, act, col, col,
            act, act, act, act, act, act, act, act,
            heads, heads,
            pltpu.VMEM((2, NZ, CHUNK, COLS), F32), chunks, chunks, pltpu.VMEM((2, CHUNK, COLS), BF), chunks, heads,
            dma((4,)), dma((4,)), dma((3,)), dma((3,)), dma((4, 4)), dma, dma((2,)), dma((2,)), dma((2,)), dma((2,)),
            dma((80,)), dma((12,)),
        ],
        compiler_params=pltpu.CompilerParams(collective_id=0, has_side_effects=True),
    )(depths, hidden, masked, gain, wq, wk, wv, wo, cot)


def body(hidden, masked, depths, norm_gain, w_query, w_key, w_value, w_out, cotangent):
    shape = hidden.shape
    tokens = (shape[1] * shape[2], shape[3])
    mixed, grad = step(depths, hidden.reshape(tokens), masked[0], norm_gain, w_query, w_key, w_value, w_out,
                       cotangent.reshape(tokens))
    return mixed.reshape(shape), grad.reshape(shape)


def solution(mesh):
    return jax.shard_map(
        body,
        mesh=mesh,
        in_specs=(
            P("dp", "row", None, None),
            P("dp", "row", None),
            P("dp"),
            P(),
            P("row", None),
            P("row", None),
            P("row", None),
            P("row", None),
            P("dp", "row", None, None),
        ),
        out_specs=(P("dp", "row", None, None), P("dp", "row", None, None)),
        check_vma=False,
    )
```
